32 devices in a mesh: row: 8 (over y, x, core), col: 4 (over z).
Axes of the slice: x: 2, y: 2, z: 4, core: 2. Of those that a mesh axis runs over, the one named last changes fastest.
Arguments:
- positions: float32 [3, 2048], P(None, ('row', 'col')), may hold values from -0.2 to 63.2, as said below
- radii: float32 [2048], P(('row', 'col')), may hold values from 0.1 to 0.28
- basis: float32 [32, 3, 2048], P(None, None, ('row', 'col')), may hold values from -0.031894398 to 0.031894398, as said below
- rhs: float32 [3, 2048], P(None, ('row', 'col')), may hold values from -6 to 6
Outputs:
- solution: float32 [3, 2048], P(None, ('row', 'col'))
- residual: float32 [3, 2048], P(None, ('row', 'col'))
The draws below stay inside these ranges and needn't reach their ends.
Inputs may be any that keep to these rules, and one draw needn't show every extreme that they name: `positions`: every coordinate lies within 0.2 of a whole number and any two centres are 0.6 or more apart, more than the sum of any two radii. `basis`: the 32 vectors are linearly independent.
All inputs are finite; a program needn't handle non-finite values.
Results may differ from the reference program's by a relative error of at most 0.0003.
Values sent between devices are 32-bit elements; how exact they have to be, the bound alone decides.
No kernel may reach another device: no remote copies, remote signals or barrier semaphores. Data moves between devices by JAX's collectives and lax.ppermute only.
A program may use at most 64 MiB of HBM per device.

```python
import math
import jax
import jax.numpy as jnp
from jax import lax

SPHERES_DEV = 64
BASIS = 32
ITERS = 2
TARGETS = 512
SOURCES = 256
SPHERES = 2048
ORDER = 6144


def lattice_points():
    sphere_index = jnp.arange(SPHERES, dtype=jnp.int32)
    piece = sphere_index // SPHERES_DEV
    columns = SOURCES // SPHERES_DEV
    coords = jnp.stack([piece // columns, piece % columns, sphere_index % SPHERES_DEV])
    return coords.astype(jnp.float32)


def lattice_extent():
    return jnp.array([TARGETS // SPHERES_DEV, SOURCES // SPHERES_DEV, SPHERES_DEV], jnp.float32)[:, None]


def draw_positions(key, part):
    points = lattice_points()
    jitter = jax.random.uniform(key, (3, SPHERES), jnp.float32, -0.2, 0.2)
    return points + jitter


def draw_basis(key, part):
    streams = jax.random.split(jax.random.fold_in(key, 11), 3)
    scaled_points = lattice_points() / lattice_extent()
    freqs = jax.random.randint(streams[0], (BASIS, 3, 3), 0, 3).astype(jnp.float32)
    phase = jax.random.uniform(streams[1], (BASIS, 3, 1), jnp.float32, 0.0, 2.0 * math.pi)
    wave = jnp.cos(2.0 * math.pi * jnp.einsum('kcd,dp->kcp', freqs, scaled_points) + phase)
    rough = jax.random.normal(streams[2], (BASIS, 3, SPHERES), jnp.float32)
    return jnp.clip(wave + 0.5 * rough, -2.5, 2.5) / math.sqrt(ORDER)


def draw_rhs(key, part):
    streams = jax.random.split(jax.random.fold_in(key, 23), 3)
    scaled_points = lattice_points() / lattice_extent()
    order_float = jnp.arange(SPHERES, dtype=jnp.int32).astype(jnp.float32)
    rising = jnp.exp(math.log(3.0) * order_float / SPHERES)
    phase = jax.random.uniform(streams[0], (3, 1), jnp.float32, 0.0, 2.0 * math.pi)
    freqs = jax.random.randint(streams[1], (3, 3), 1, 3).astype(jnp.float32)
    wave = jnp.cos(2.0 * math.pi * jnp.einsum('cd,dp->cp', freqs, scaled_points) + phase)
    rough = jnp.clip(jax.random.normal(streams[2], (3, SPHERES), jnp.float32), -4.0, 4.0)
    value = 0.5 * rising * (rough + wave)
    return jnp.clip(value, -6.0, 6.0)


def steps_of(rng, shape, cuts, low, top_value):
    def one(axis_at, parts):
        heights = jax.random.uniform(jax.random.fold_in(jax.random.fold_in(rng, 6), axis_at), (parts,), jnp.float32, low / len(cuts), top_value / len(cuts))
        return jnp.repeat(jnp.exp(heights), shape[axis_at] // parts).reshape((-1,) + (1,) * (len(shape) - axis_at - 1))

    level = one(*cuts[0])
    for cut in cuts[1:]:
        level = level * one(*cut)
    return level


def setup_inputs(seed: int = 0) -> dict:
    streams_of = jax.random.split(jax.random.key(seed), 5)
    return {
        "positions": draw_positions(jax.random.fold_in(streams_of[4], 71), 0),
        "radii": jnp.clip(jnp.exp(math.log(0.28) - 1.0296194 * jax.random.uniform(streams_of[1], (SPHERES,), jnp.float32) ** steps_of(streams_of[1], (SPHERES,), ((0, 32),), -0.2, 0.2)), 0.1, 0.28),
        "basis": draw_basis(jax.random.fold_in(streams_of[4], 71), 0),
        "rhs": draw_rhs(jax.random.fold_in(streams_of[4], 71), 0),
    }


far_scale = 1.0 / (8.0 * math.pi)
self_scale = 1.0 / (6.0 * math.pi)
highest = lax.Precision.HIGHEST

def contract(left, right):
    return lax.dot_general(left.astype(jnp.float32), right.astype(jnp.float32), (((1,), (1,)), ((), ())), precision=highest, preferred_element_type=jnp.float32)

def block_apply(out_pos, out_rad, out_index, in_pos, in_rad, in_index, fields):
    deltas = [out_pos[axis_id][:, None] - in_pos[axis_id][None, :] for axis_id in range(3)]
    coincide = out_index[:, None] == in_index[None, :]
    dist_sq = deltas[0] * deltas[0] + deltas[1] * deltas[1] + deltas[2] * deltas[2]
    safe_sq = jnp.where(coincide, jnp.ones_like(dist_sq), dist_sq)
    inv_sq = 1.0 / safe_sq
    inv_dist = jnp.sqrt(inv_sq)
    radius_sum = (out_rad * out_rad)[:, None] + (in_rad * in_rad)[None, :]
    scaled = far_scale * inv_dist
    isotropic = scaled * (1.0 + radius_sum * inv_sq / 3.0)
    own_term = jnp.broadcast_to((self_scale / out_rad)[:, None], isotropic.shape)
    isotropic = jnp.where(coincide, own_term, isotropic)
    along = jnp.where(coincide, jnp.zeros_like(dist_sq), scaled * (1.0 - radius_sum * inv_sq) * inv_sq)
    tensors = {}
    for first in range(3):
        for second in range(first, 3):
            entry = along * deltas[first] * deltas[second]
            if first == second:
                entry = entry + isotropic
            tensors[first, second] = entry
    results = []
    for first in range(3):
        total = None
        for second in range(3):
            term = contract(fields[:, second, :], tensors[min(first, second), max(first, second)])
            total = term if total is None else total + term
        results.append(total)
    return jnp.stack(results, axis=1)

def field_apply(out_pos, out_rad, out_index, in_pos, in_rad, in_index, fields, width):
    count = out_rad.shape[0] // width
    pos_blocks = out_pos.reshape(3, count, width).transpose(1, 0, 2)
    rad_blocks = out_rad.reshape(count, width)
    index_blocks = out_index.reshape(count, width)

    def one_block(packed):
        return block_apply(packed[0], packed[1], packed[2], in_pos, in_rad, in_index, fields)
    stacked = lax.map(one_block, (pos_blocks, rad_blocks, index_blocks))
    return stacked.transpose(1, 2, 0, 3).reshape(fields.shape[0], 3, count * width)

def reference(positions, radii, basis, rhs):
    sphere_index = jnp.arange(SPHERES, dtype=jnp.int32)

    def mobility(fields):
        return field_apply(positions, radii, sphere_index, positions, radii, sphere_index, fields, SPHERES_DEV)
    basis_image = mobility(basis)
    gram = jnp.einsum('kcp,lcp->kl', basis, basis_image, precision=highest)
    load = jnp.einsum('kcp,cp->k', basis, rhs, precision=highest)
    factor = jnp.linalg.cholesky(gram)

    def coarse_solve(vector):
        return jax.scipy.linalg.cho_solve((factor, True), vector)
    coarse = coarse_solve(load)
    solution = jnp.einsum('k,kcp->cp', coarse, basis, precision=highest)
    residual = rhs - jnp.einsum('k,kcp->cp', coarse, basis_image, precision=highest)
    norm_now = jnp.sum(residual * residual)
    projection = coarse_solve(jnp.einsum('kcp,cp->k', basis_image, residual, precision=highest))
    direction = residual - jnp.einsum('k,kcp->cp', projection, basis, precision=highest)
    for iteration in range(ITERS):
        image = mobility(direction[None])[0]
        step_size = norm_now / jnp.sum(direction * image)
        solution = solution + step_size * direction
        residual = residual - step_size * image
        if iteration + 1 < ITERS:
            norm_next = jnp.sum(residual * residual)
            projection = coarse_solve(jnp.einsum('kcp,cp->k', basis_image, residual, precision=highest))
            direction = residual + norm_next / norm_now * direction - jnp.einsum('k,kcp->cp', projection, basis, precision=highest)
            norm_now = norm_next
    return (solution, residual)
```

```python
import functools
import math

import jax
import jax.numpy as jnp
from jax import lax
from jax.experimental import pallas as pl
from jax.experimental.pallas import tpu as pltpu
from jax.sharding import PartitionSpec as P

ITERS = 2
LANES = 128
AXES = ("row", "col")

far_scale = 1.0 / (8.0 * math.pi)
self_scale = 1.0 / (6.0 * math.pi)
highest = lax.Precision.HIGHEST


def nt_dot(left, right):
    return lax.dot_general(
        left, right, (((1,), (1,)), ((), ())), precision=highest, preferred_element_type=jnp.float32
    )


def join_lanes(left, right):
    return jnp.concatenate([left, right], axis=1)


def run_blocks(count, body):
    if count <= 16:
        for index in range(count):
            body(index)
    else:

        @pl.loop(0, count)
        def _(index):
            body(index)


def low_half(shape):
    return lax.broadcasted_iota(jnp.int32, shape, 1) < LANES // 2


def pack_kernel(pos_ref, rad_ref, basis_ref, rhs_ref, out_ref):
    vectors = basis_ref.shape[1]
    half = vectors // 2
    for axis_id in range(3):
        piece = basis_ref[axis_id]
        out_ref[pl.ds(axis_id * half, half), :] = join_lanes(piece[:half], piece[half:])
    rows = jnp.concatenate(
        [pos_ref[...], rad_ref[...], rhs_ref[...], jnp.zeros_like(rad_ref[...])], axis=0
    )
    out_ref[pl.ds(3 * half, 8), :] = join_lanes(rows, rows)


def unpack_basis(first, second, half):
    low = low_half((half, LANES))
    upper = jnp.where(low, first, pltpu.roll(second, LANES // 2, 1))
    lower = jnp.where(low, pltpu.roll(first, LANES // 2, 1), second)
    return jnp.concatenate([upper, lower], axis=0)


def image_kernel(
    gathered_ref, image_ref, iso_ref, along_ref, basis_ref, info_ref, column_ref, tensor_ref
):
    blocks = iso_ref.shape[0]
    half = basis_ref.shape[2] // 2
    width = iso_ref.shape[1]
    low8 = low_half((8, LANES))
    columns = jnp.transpose(
        jnp.concatenate(
            [gathered_ref[0, pl.ds(3 * half, 8), :], jnp.zeros((LANES - 8, LANES), jnp.float32)], axis=0
        )
    )
    column_ref[...] = columns[:width]

    def build(index, slot):
        first = gathered_ref.at[2 * index]
        second = gathered_ref.at[2 * index + 1]
        for axis_id in range(3):
            rows = pl.ds(axis_id * half, half)
            basis_ref[index, axis_id] = unpack_basis(first[rows, :], second[rows, :], half)
        rows = pl.ds(3 * half, 8)
        info_ref[index] = jnp.where(low8, first[rows, :], second[rows, :])
        for group in range(width // 8):
            rows = pl.ds(group * 8, 8)
            target = [column_ref[rows, pl.ds(entry, 1)] for entry in range(4)]
            source = [info_ref[index, pl.ds(entry, 1), :] for entry in range(4)]
            deltas = [target[entry] - source[entry] for entry in range(3)]
            dist_sq = deltas[0] * deltas[0] + deltas[1] * deltas[1] + deltas[2] * deltas[2]
            own = isinstance(index, int) and index == 0
            check = own or not isinstance(index, int)
            if check:
                lane = lax.broadcasted_iota(jnp.int32, (8, LANES), 1)
                row = lax.broadcasted_iota(jnp.int32, (8, LANES), 0) + group * 8
                coincide = (lane == row) if own else ((lane == row) & (index == 0))
                dist_sq = jnp.where(coincide, 1.0, dist_sq)
            inv_dist = lax.rsqrt(dist_sq)
            inv_sq = inv_dist * inv_dist
            radius_sum = target[3] * target[3] + source[3] * source[3]
            scaled = far_scale * inv_dist
            ratio = radius_sum * inv_sq
            isotropic = scaled * (1.0 + ratio * (1.0 / 3.0))
            along = scaled * (1.0 - ratio) * inv_sq
            if check:
                isotropic = jnp.where(coincide, self_scale / target[3], isotropic)
                along = jnp.where(coincide, 0.0, along)
            iso_ref[index, rows, :] = isotropic
            along_ref[index, rows, :] = along
            for one in range(3):
                for two in range(one, 3):
                    entry = along * deltas[one] * deltas[two]
                    if one == two:
                        entry = entry + isotropic
                    for out_axis, in_axis in {(one, two), (two, one)}:
                        tensor_ref[
                            pl.ds(out_axis * width + group * 8, 8),
                            pl.ds(in_axis * 2 * LANES + slot * LANES, LANES),
                        ] = entry

    image_ref[...] = jnp.zeros_like(image_ref)

    def chunk(index):
        build(2 * index, 0)
        build(2 * index + 1, 1)
        fields = jnp.concatenate(
            [basis_ref[2 * index + slot, axis_id] for axis_id in range(3) for slot in range(2)], axis=1
        )
        image_ref[...] += nt_dot(fields, tensor_ref[...])

    run_blocks(blocks // 2, chunk)


def pack_image_kernel(image_ref, out_ref):
    half = image_ref.shape[0] // 2
    width = image_ref.shape[1] // 3
    image = image_ref[...]
    for axis_id in range(3):
        piece = image[:, axis_id * width : (axis_id + 1) * width]
        out_ref[pl.ds(axis_id * half, half), :] = join_lanes(piece[:half], piece[half:])


def column_of(row, identity):
    return jnp.sum(identity * row, axis=1, keepdims=True)


def row_of(column, identity):
    return jnp.sum(identity * column, axis=0, keepdims=True)


def invert(matrix):
    order = matrix.shape[0]
    lane = lax.broadcasted_iota(jnp.int32, (order, order), 1)
    sub = lax.broadcasted_iota(jnp.int32, (order, order), 0)
    for step in range(order):
        pivot_row = matrix[step : step + 1, :]
        pivot_col = matrix[:, step : step + 1]
        scale = 1.0 / matrix[step : step + 1, step : step + 1]
        scaled_row = jnp.where(lane[:1] == step, 1.0, pivot_row) * scale
        others = jnp.where(lane == step, 0.0, matrix) - pivot_col * scaled_row
        matrix = jnp.where(sub == step, scaled_row, others)
    return matrix


def product_rows(iso_ref, along_ref, info_ref, column_ref, field_ref, acc_ref):
    blocks, width, _ = iso_ref.shape
    acc_ref[...] = jnp.zeros_like(acc_ref)

    def block(index):
        for group in range(width // 8):
            rows = pl.ds(group * 8, 8)
            deltas = [
                column_ref[rows, pl.ds(entry, 1)] - info_ref[index, pl.ds(entry, 1), :] for entry in range(3)
            ]
            field = [field_ref[index, pl.ds(entry, 1), :] for entry in range(3)]
            inner = deltas[0] * field[0] + deltas[1] * field[1] + deltas[2] * field[2]
            inner = inner * along_ref[index, rows, :]
            isotropic = iso_ref[index, rows, :]
            for entry in range(3):
                acc_ref[entry, rows, :] += isotropic * field[entry] + inner * deltas[entry]

    run_blocks(blocks, block)


def rows_of_sums(acc_ref):
    width = acc_ref.shape[1]
    ones = jnp.ones((8, LANES), jnp.float32)
    parts = [nt_dot(ones, acc_ref[entry]) for entry in range(3)]
    sub = lax.broadcasted_iota(jnp.int32, (8, width), 0)
    rows = jnp.where(sub == 0, parts[0], jnp.where(sub == 1, parts[1], jnp.where(sub == 2, parts[2], 0.0)))
    return join_lanes(rows, rows)


def correlate(image_ref, field_ref, blocks):
    total = None
    for index in range(blocks):
        for axis_id in range(3):
            term = image_ref[index, axis_id] * field_ref[index, pl.ds(axis_id, 1), :]
            total = term if total is None else total + term
    return jnp.sum(total, axis=1, keepdims=True)


def blocks_dot(left_ref, right_ref, blocks):
    total = None
    for index in range(blocks):
        term = left_ref[index, pl.ds(0, 3), :] * right_ref[index, pl.ds(0, 3), :]
        total = term if total is None else total + term
    return jnp.sum(jnp.sum(total, axis=1, keepdims=True), axis=0, keepdims=True)


def combine(column, fields_ref, index, axis_id):
    return jnp.sum(column * fields_ref[index, axis_id], axis=0, keepdims=True)


def first_kernel(
    gathered_ref, iso_ref, along_ref, basis_ref, info_ref, column_ref,
    rows_ref, image_ref, residual_ref, direction_ref, own_ref, inverse_ref, norm_ref, acc_ref,
):
    blocks = iso_ref.shape[0]
    vectors = basis_ref.shape[2]
    half = vectors // 2
    gram = jnp.zeros((vectors, vectors), jnp.float32)
    load = jnp.zeros((vectors, LANES), jnp.float32)
    for index in range(blocks):
        for axis_id in range(3):
            rows = pl.ds(axis_id * half, half)
            image_ref[index, axis_id] = unpack_basis(
                gathered_ref[2 * index, rows, :], gathered_ref[2 * index + 1, rows, :], half
            )
            load = load + basis_ref[index, axis_id] * info_ref[index, pl.ds(4 + axis_id, 1), :]
    for index in range(blocks // 2):
        left = [basis_ref[2 * index + slot, axis_id] for axis_id in range(3) for slot in range(2)]
        right = [image_ref[2 * index + slot, axis_id] for axis_id in range(3) for slot in range(2)]
        gram = gram + nt_dot(jnp.concatenate(left, axis=1), jnp.concatenate(right, axis=1))
    identity = jnp.where(
        lax.broadcasted_iota(jnp.int32, gram.shape, 0) == lax.broadcasted_iota(jnp.int32, gram.shape, 1), 1.0, 0.0
    )
    inverse = invert(gram)
    inverse_ref[...] = inverse

    def coarse_solve(column):
        return jnp.sum(inverse * row_of(column, identity), axis=1, keepdims=True)

    coarse = coarse_solve(jnp.sum(load, axis=1, keepdims=True))
    for index in range(blocks):
        for axis_id in range(3):
            residual_ref[index, pl.ds(axis_id, 1), :] = info_ref[index, pl.ds(4 + axis_id, 1), :] - combine(
                coarse, image_ref, index, axis_id
            )
    norm_ref[...] = jnp.broadcast_to(blocks_dot(residual_ref, residual_ref, blocks), norm_ref.shape)
    projection = coarse_solve(correlate(image_ref, residual_ref, blocks))
    for index in range(blocks):
        for axis_id in range(3):
            row = pl.ds(axis_id, 1)
            direction_ref[index, row, :] = residual_ref[index, row, :] - combine(
                projection, basis_ref, index, axis_id
            )
    for axis_id in range(3):
        own_ref[pl.ds(axis_id, 1), :] = combine(coarse, basis_ref, 0, axis_id)
    product_rows(iso_ref, along_ref, info_ref, column_ref, direction_ref, acc_ref)
    rows = rows_of_sums(acc_ref)[:4]
    rows_ref[...] = jnp.broadcast_to(rows[None], rows_ref.shape)


def second_kernel(
    bits_ref, gathered_ref, iso_ref, along_ref, basis_ref, info_ref, column_ref, image_ref, residual_ref,
    direction_ref, own_ref, inverse_ref, norm_ref,
    partial_ref, state_ref, product_ref, next_ref, later_ref, acc_ref, *, cols,
):
    blocks = iso_ref.shape[0]
    vectors = basis_ref.shape[2]
    row_id = bits_ref[0]
    col_id = bits_ref[1]
    row_half = gathered_ref.shape[0] // cols // 2
    low = low_half((4, LANES))

    def place(piece):
        other_row = piece // cols
        core, rest = other_row // row_half, other_row % row_half
        return (row_id ^ (2 * rest + core)) * cols + (col_id ^ (piece % cols))

    for index in range(blocks):
        product_ref[index] = jnp.where(
            low, gathered_ref[place(2 * index)], gathered_ref[place(2 * index + 1)]
        )
    norm_now = norm_ref[pl.ds(0, 1), pl.ds(0, 1)]
    step_size = norm_now / blocks_dot(direction_ref, product_ref, blocks)
    for index in range(blocks):
        next_ref[index, pl.ds(0, 3), :] = (
            residual_ref[index, pl.ds(0, 3), :] - step_size * product_ref[index, pl.ds(0, 3), :]
        )
    norm_next = blocks_dot(next_ref, next_ref, blocks)
    identity = jnp.where(
        lax.broadcasted_iota(jnp.int32, (vectors, vectors), 0)
        == lax.broadcasted_iota(jnp.int32, (vectors, vectors), 1),
        1.0,
        0.0,
    )
    correlation = correlate(image_ref, next_ref, blocks)
    projection = jnp.sum(inverse_ref[...] * row_of(correlation, identity), axis=1, keepdims=True)
    momentum = norm_next / norm_now
    for index in range(blocks):
        for axis_id in range(3):
            row = pl.ds(axis_id, 1)
            later_ref[index, row, :] = (
                next_ref[index, row, :]
                + momentum * direction_ref[index, row, :]
                - combine(projection, basis_ref, index, axis_id)
            )
    product_rows(iso_ref, along_ref, info_ref, column_ref, later_ref, acc_ref)
    rows = rows_of_sums(acc_ref)
    width = iso_ref.shape[1]
    ours = lax.broadcasted_iota(jnp.int32, (3, LANES), 1) < width
    inner = jnp.where(ours, later_ref[0, pl.ds(0, 3), :] * rows[:3], 0.0)
    partial = jnp.sum(jnp.sum(inner, axis=1, keepdims=True), axis=0, keepdims=True)
    partial_ref[...] = jnp.broadcast_to(partial[None], partial_ref.shape)
    state_ref[pl.ds(0, 3), :] = own_ref[pl.ds(0, 3), :] + step_size * direction_ref[0, pl.ds(0, 3), :]
    state_ref[pl.ds(3, 3), :] = later_ref[0, pl.ds(0, 3), :]
    state_ref[pl.ds(6, 3), :] = next_ref[0, pl.ds(0, 3), :]
    state_ref[pl.ds(9, 3), :] = rows[:3]
    state_ref[pl.ds(12, 4), :] = jnp.broadcast_to(norm_next, (4, LANES))


def last_kernel(partial_ref, state_ref, solution_ref, residual_ref):
    width = solution_ref.shape[1]
    total = jnp.sum(partial_ref[...], axis=0)[:, :1]
    step_size = state_ref[pl.ds(12, 1), pl.ds(0, 1)] / total
    moved = state_ref[pl.ds(0, 3), :] + step_size * state_ref[pl.ds(3, 3), :]
    left = state_ref[pl.ds(6, 3), :] - step_size * state_ref[pl.ds(9, 3), :]
    solution_ref[...] = moved[:, :width]
    residual_ref[...] = left[:, :width]


def gather_pieces(piece, rows, cols):
    def spread(stack, axis_name, size, offsets):
        parts = [stack]
        for offset in offsets:
            parts.append(lax.ppermute(stack, axis_name, [(i, i ^ offset) for i in range(size)]))
        return jnp.concatenate(parts, axis=0)

    stack = spread(piece[None], "col", cols, range(1, cols))
    stack = spread(stack, "row", rows, range(2, rows, 2))
    return spread(stack, "row", rows, (1,))


def exchange(stack):
    return lax.all_to_all(stack, AXES, 0, 0, tiled=True)


def body(positions, radii, basis, rhs):
    rows, cols = lax.axis_size("row"), lax.axis_size("col")
    devices = rows * cols
    blocks = devices // 2
    width = positions.shape[1]
    vectors = basis.shape[0]
    half = vectors // 2
    vmem = pl.BlockSpec(memory_space=pltpu.VMEM)
    smem = pl.BlockSpec(memory_space=pltpu.SMEM)

    def shaped(*shape):
        return jax.ShapeDtypeStruct(shape, jnp.float32)

    def call(kernel, name, outs, args, scratch=(), first=vmem):
        return pl.pallas_call(
            kernel,
            name=name,
            out_shape=outs,
            in_specs=[first] + [vmem] * (len(args) - 1),
            out_specs=jax.tree.map(lambda _: vmem, outs),
            scratch_shapes=list(scratch),
        )(*args)

    packed = call(
        pack_kernel,
        "pack_inputs",
        shaped(3 * half + 8, LANES),
        (positions, radii[None], basis.transpose(1, 0, 2), rhs),
    )
    gathered = gather_pieces(packed, rows, cols)
    partial_image, iso, along, fields, info, column = call(
        image_kernel,
        "basis_image",
        (
            shaped(vectors, 3 * width),
            shaped(blocks, width, LANES),
            shaped(blocks, width, LANES),
            shaped(blocks, 3, vectors, LANES),
            shaped(blocks, 8, LANES),
            shaped(width, LANES),
        ),
        (gathered,),
        [pltpu.VMEM((3 * width, 6 * LANES), jnp.float32)],
    )
    packed_image = call(pack_image_kernel, "pack_image", shaped(3 * half, LANES), (partial_image,))
    gathered_image = gather_pieces(packed_image, rows, cols)
    product, image, residual, direction, own, inverse, norm = call(
        first_kernel,
        "first_product",
        (
            shaped(devices, 4, LANES),
            shaped(blocks, 3, vectors, LANES),
            shaped(blocks, 4, LANES),
            shaped(blocks, 4, LANES),
            shaped(4, LANES),
            shaped(vectors, vectors),
            shaped(8, LANES),
        ),
        (gathered_image, iso, along, fields, info, column),
        [pltpu.VMEM((3, width, LANES), jnp.float32)],
    )
    product = exchange(product)
    bits = jnp.stack([lax.axis_index("row"), lax.axis_index("col")]).astype(jnp.int32)
    partial, state = call(
        functools.partial(second_kernel, cols=cols),
        "second_product",
        (shaped(devices, 1, LANES), shaped(16, LANES)),
        (bits, product, iso, along, fields, info, column, image, residual, direction, own, inverse, norm),
        [
            pltpu.VMEM((blocks, 4, LANES), jnp.float32),
            pltpu.VMEM((blocks, 4, LANES), jnp.float32),
            pltpu.VMEM((blocks, 4, LANES), jnp.float32),
            pltpu.VMEM((3, width, LANES), jnp.float32),
        ],
        first=smem,
    )
    partial = exchange(partial)
    return call(last_kernel, "last_step", (shaped(3, width), shaped(3, width)), (partial, state))


def solution(mesh):
    return jax.shard_map(
        body,
        mesh=mesh,
        in_specs=(
            P(None, AXES),
            P(AXES),
            P(None, None, AXES),
            P(None, AXES),
        ),
        out_specs=(P(None, AXES), P(None, AXES)),
        check_vma=False,
    )
```

```python
import functools
import math

import jax
import jax.numpy as jnp
from jax import lax
from jax.experimental import pallas as pl
from jax.experimental.pallas import tpu as pltpu
from jax.sharding import PartitionSpec as P

ITERS = 2
LANES = 128
AXES = ("row", "col")

far_scale = 1.0 / (8.0 * math.pi)
self_scale = 1.0 / (6.0 * math.pi)
highest = lax.Precision.HIGHEST


def nt_dot(left, right, precision=highest):
    return lax.dot_general(
        left, right, (((1,), (1,)), ((), ())), precision=precision, preferred_element_type=jnp.float32
    )


def join_lanes(left, right):
    return jnp.concatenate([left, right], axis=1)


def low_half(shape):
    return lax.broadcasted_iota(jnp.int32, shape, 1) < LANES // 2


def run_blocks(count, body, carry=None):
    if count <= 16:
        for index in range(count):
            carry = body(index, carry)
        return carry
    return lax.fori_loop(0, count, body, carry)


def split(value, parts):
    pieces = []
    for part in range(parts):
        piece = value.astype(jnp.bfloat16)
        pieces.append(piece)
        if part + 1 < parts:
            value = value - piece.astype(jnp.float32)
    return pieces


def pack_kernel(pos_ref, rad_ref, basis_ref, rhs_ref, out_ref, rows_ref, fields_ref, sems):
    copies = [
        pltpu.make_async_copy(source, target, sems.at[index])
        for index, (source, target) in enumerate(
            (
                (basis_ref, fields_ref),
                (pos_ref, rows_ref.at[pl.ds(0, 3)]),
                (rad_ref, rows_ref.at[pl.ds(3, 1)]),
                (rhs_ref, rows_ref.at[pl.ds(4, 3)]),
            )
        )
    ]
    for copy in copies:
        copy.start()
    for copy in copies:
        copy.wait()
    half = fields_ref.shape[1] // 2
    for axis_id in range(3):
        piece = fields_ref[axis_id]
        out_ref[pl.ds(axis_id * half, half), :] = join_lanes(piece[:half], piece[half:])
    rows_ref[pl.ds(7, 1), :] = rows_ref[pl.ds(3, 1), :] * rows_ref[pl.ds(3, 1), :]
    rows = rows_ref[...]
    out_ref[pl.ds(3 * half, 8), :] = join_lanes(rows, rows)


def unpack_basis(first, second, half):
    low = low_half((half, LANES))
    upper = jnp.where(low, first, pltpu.roll(second, LANES // 2, 1))
    lower = jnp.where(low, pltpu.roll(first, LANES // 2, 1), second)
    return jnp.concatenate([upper, lower], axis=0)


def chunk_of(ref, index):
    return jnp.concatenate(
        [ref[2 * index + slot, axis_id] for axis_id in range(3) for slot in range(2)], axis=1
    )


def image_kernel(*refs, own):
    if own:
        gathered_ref, part_ref, iso_ref, along_ref, basis_ref, split_ref, info_ref, column_ref = refs[:8]
    else:
        gathered_ref, before_ref, column_ref = refs[:3]
        packed_ref, iso_ref, along_ref, basis_ref, split_ref, info_ref, part_ref = refs[3:10]
    high_ref, rest_ref = refs[-2:]
    blocks, width, _ = iso_ref.shape
    half = basis_ref.shape[2] // 2
    low8 = low_half((8, LANES))
    if own:
        columns = jnp.transpose(
            jnp.concatenate(
                [gathered_ref[0, pl.ds(3 * half, 8), :], jnp.zeros((LANES - 8, LANES), jnp.float32)], axis=0
            )
        )
        for slot, entry in enumerate((0, 1, 2, 7, 3)):
            column_ref[slot] = jnp.broadcast_to(columns[:width, entry : entry + 1], (width, LANES))
        part_ref[...] = jnp.zeros_like(part_ref)
    else:
        part_ref[...] = before_ref[...]

    def build(index, slot):
        first = gathered_ref.at[2 * index]
        second = gathered_ref.at[2 * index + 1]
        for axis_id in range(3):
            rows = pl.ds(axis_id * half, half)
            basis_ref[index, axis_id] = unpack_basis(first[rows, :], second[rows, :], half)
        rows = pl.ds(3 * half, 8)
        info_ref[index] = jnp.where(low8, first[rows, :], second[rows, :])
        source = [info_ref[index, pl.ds(entry, 1), :] for entry in (0, 1, 2, 7)]
        for group in range(width // 16):
            rows = pl.ds(group * 16, 16)
            deltas = [column_ref[entry, rows, :] - source[entry] for entry in range(3)]
            dist_sq = deltas[0] * deltas[0] + deltas[1] * deltas[1] + deltas[2] * deltas[2]
            check = own and not (isinstance(index, int) and index > 0)
            if check:
                lane = lax.broadcasted_iota(jnp.int32, (16, LANES), 1)
                row = lax.broadcasted_iota(jnp.int32, (16, LANES), 0) + group * 16
                coincide = lane == row
                if not isinstance(index, int):
                    coincide = coincide & (index == 0)
                dist_sq = jnp.where(coincide, 1.0, dist_sq)
            inv_dist = lax.rsqrt(dist_sq)
            inv_sq = inv_dist * inv_dist
            scaled = far_scale * inv_dist
            ratio = (column_ref[3, rows, :] + source[3]) * inv_sq
            isotropic = scaled + scaled * (ratio * (1.0 / 3.0))
            along = (scaled - scaled * ratio) * inv_sq
            if check:
                isotropic = jnp.where(coincide, self_scale / column_ref[4, rows, :], isotropic)
                along = jnp.where(coincide, 0.0, along)
            iso_ref[index, rows, :] = isotropic
            along_ref[index, rows, :] = along
            for one in range(3):
                leaning = along * deltas[one]
                for two in range(one, 3):
                    entry = leaning * deltas[two]
                    if one == two:
                        entry = entry + isotropic
                    pieces = split(entry, 2)
                    for out_axis, in_axis in sorted({(one, two), (two, one)}):
                        place = (
                            pl.ds(out_axis * width + group * 16, 16),
                            pl.ds((in_axis * 2 + slot) * LANES, LANES),
                        )
                        high_ref[place] = pieces[0]
                        rest_ref[place] = pieces[1]

    def chunk(index, _):
        build(2 * index, 0)
        build(2 * index + 1, 1)
        fields = jnp.concatenate(split(chunk_of(basis_ref, index), 3), axis=0)
        split_ref[index] = fields
        part_ref[...] += nt_dot(fields, high_ref[...], None) + nt_dot(fields, rest_ref[...], None)
        return _

    run_blocks(blocks // 2, chunk, 0)
    if not own:
        total = part_ref[...]
        image = total[: 2 * half] + total[2 * half : 4 * half] + total[4 * half :]
        for axis_id in range(3):
            piece = image[:, axis_id * width : (axis_id + 1) * width]
            packed_ref[pl.ds(axis_id * half, half), :] = join_lanes(piece[:half], piece[half:])


def row_of(column, identity):
    return jnp.sum(identity * column, axis=0, keepdims=True)


def identity_of(order):
    return jnp.where(
        lax.broadcasted_iota(jnp.int32, (order, order), 0) == lax.broadcasted_iota(jnp.int32, (order, order), 1),
        1.0,
        0.0,
    )


def invert(matrix):
    order = matrix.shape[0]
    lane = lax.broadcasted_iota(jnp.int32, (order, order), 1)
    sub = lax.broadcasted_iota(jnp.int32, (order, order), 0)
    for step in range(order):
        pivot_row = matrix[step : step + 1, :]
        pivot_col = matrix[:, step : step + 1]
        scale = 1.0 / matrix[step : step + 1, step : step + 1]
        scaled_row = jnp.where(lane[:1] == step, 1.0, pivot_row) * scale
        others = jnp.where(lane == step, 0.0, matrix) - pivot_col * scaled_row
        matrix = jnp.where(sub == step, scaled_row, others)
    return matrix


def product_rows(pairs, column_ref, acc_ref):
    width = column_ref.shape[1]
    totals = tuple(jnp.zeros((width, LANES), jnp.float32) for _ in range(3))
    for iso_ref, along_ref, info_ref, field_ref in pairs:

        def block(index, sums):
            deltas = [column_ref[entry] - info_ref[index, pl.ds(entry, 1), :] for entry in range(3)]
            field = [field_ref[index, pl.ds(entry, 1), :] for entry in range(3)]
            inner = deltas[0] * field[0] + deltas[1] * field[1] + deltas[2] * field[2]
            inner = inner * along_ref[index]
            isotropic = iso_ref[index]
            return tuple(sums[entry] + (isotropic * field[entry] + inner * deltas[entry]) for entry in range(3))

        totals = run_blocks(iso_ref.shape[0], block, totals)
    for entry in range(3):
        acc_ref[entry] = totals[entry]


def rows_of_sums(acc_ref):
    width = acc_ref.shape[1]
    ones = jnp.ones((8, LANES), jnp.float32)
    parts = [nt_dot(ones, acc_ref[entry]) for entry in range(3)]
    sub = lax.broadcasted_iota(jnp.int32, (8, width), 0)
    rows = jnp.where(sub == 0, parts[0], jnp.where(sub == 1, parts[1], jnp.where(sub == 2, parts[2], 0.0)))
    return join_lanes(rows, rows)


def correlate(pairs):
    total = None
    for image_ref, field_ref, row in pairs:

        def block(index, carry):
            for axis_id in range(3):
                carry = carry + image_ref[index, axis_id] * field_ref[index, pl.ds(row + axis_id, 1), :]
            return carry

        if total is None:
            total = jnp.zeros((image_ref.shape[2], LANES), jnp.float32)
        total = run_blocks(image_ref.shape[0], block, total)
    return total


def lane_sum(value):
    return jnp.sum(value, axis=1, keepdims=True)


def fields_dot(pairs):
    total = jnp.zeros((3, LANES), jnp.float32)
    for left_ref, right_ref in pairs:

        def block(index, carry):
            return carry + left_ref[index, pl.ds(0, 3), :] * right_ref[index, pl.ds(0, 3), :]

        total = run_blocks(left_ref.shape[0], block, total)
    return jnp.sum(lane_sum(total), axis=0, keepdims=True)


def combine(column, fields_ref, index):
    return jnp.concatenate(
        [jnp.sum(column * fields_ref[index, axis_id], axis=0, keepdims=True) for axis_id in range(3)], axis=0
    )


def gram_kernel(gathered_ref, split_ref, *refs, own):
    if own:
        basis_refs, info_refs = refs[:2], refs[2:4]
        image_ref, part_ref, load_ref = refs[4:7]
    else:
        image_ref, part_ref = refs
    blocks = image_ref.shape[0]
    vectors = image_ref.shape[2]
    half = vectors // 2

    def chunk(index, carry):
        for slot in range(2):
            for axis_id in range(3):
                rows = pl.ds(axis_id * half, half)
                image_ref[2 * index + slot, axis_id] = unpack_basis(
                    gathered_ref[4 * index + 2 * slot, rows, :],
                    gathered_ref[4 * index + 2 * slot + 1, rows, :],
                    half,
                )
        images = jnp.concatenate(split(chunk_of(image_ref, index), 3), axis=0)
        return carry + nt_dot(split_ref[index], images, None)

    part_ref[...] = run_blocks(blocks // 2, chunk, jnp.zeros((3 * vectors, 3 * vectors), jnp.float32))
    if own:
        load_ref[...] = correlate([(basis_refs[0], info_refs[0], 4), (basis_refs[1], info_refs[1], 4)])


def first_kernel(
    gathered_ref, split_ref, before_ref, load_ref, image_a_ref, basis_a_ref, basis_b_ref, info_a_ref, info_b_ref,
    iso_a_ref, iso_b_ref, along_a_ref, along_b_ref, column_ref,
    rows_ref, image_b_ref, residual_a_ref, residual_b_ref, direction_a_ref, direction_b_ref, own_ref, inverse_ref,
    norm_ref, correlation_ref, part_ref, acc_ref,
):
    vectors = basis_a_ref.shape[2]
    gram_kernel(gathered_ref, split_ref, image_b_ref, part_ref, own=False)
    part = part_ref[...] + before_ref[...]
    part = part[:vectors] + part[vectors : 2 * vectors] + part[2 * vectors :]
    gram = part[:, :vectors] + part[:, vectors : 2 * vectors] + part[:, 2 * vectors :]
    identity = identity_of(vectors)
    inverse = invert(gram)
    inverse_ref[...] = inverse

    def coarse_solve(column):
        return lane_sum(inverse * row_of(column, identity))

    coarse = coarse_solve(lane_sum(load_ref[...]))
    halves = (
        (image_a_ref, basis_a_ref, info_a_ref, residual_a_ref, direction_a_ref),
        (image_b_ref, basis_b_ref, info_b_ref, residual_b_ref, direction_b_ref),
    )
    for image_ref, _, info_ref, residual_ref, _ in halves:

        def remain(index, carry):
            residual_ref[index, pl.ds(0, 3), :] = info_ref[index, pl.ds(4, 3), :] - combine(
                coarse, image_ref, index
            )
            return carry

        run_blocks(image_ref.shape[0], remain, 0)
    norm_ref[...] = jnp.broadcast_to(
        fields_dot([(residual_a_ref, residual_a_ref), (residual_b_ref, residual_b_ref)]), norm_ref.shape
    )
    correlation = lane_sum(correlate([(image_a_ref, residual_a_ref, 0), (image_b_ref, residual_b_ref, 0)]))
    correlation_ref[...] = jnp.broadcast_to(correlation, correlation_ref.shape)
    projection = coarse_solve(correlation)
    for _, basis_ref, _, residual_ref, direction_ref in halves:

        def point(index, carry):
            direction_ref[index, pl.ds(0, 3), :] = residual_ref[index, pl.ds(0, 3), :] - combine(
                projection, basis_ref, index
            )
            return carry

        run_blocks(basis_ref.shape[0], point, 0)
    own_ref[pl.ds(0, 3), :] = combine(coarse, basis_a_ref, 0)
    product_rows(
        [
            (iso_a_ref, along_a_ref, info_a_ref, direction_a_ref),
            (iso_b_ref, along_b_ref, info_b_ref, direction_b_ref),
        ],
        column_ref,
        acc_ref,
    )
    rows = rows_of_sums(acc_ref)[:4]
    rows_ref[...] = jnp.broadcast_to(rows[None], rows_ref.shape)


def second_kernel(
    gathered_ref, image_a_ref, image_b_ref, basis_a_ref, basis_b_ref, info_a_ref, info_b_ref,
    iso_a_ref, iso_b_ref, along_a_ref, along_b_ref, column_ref,
    residual_a_ref, residual_b_ref, direction_a_ref, direction_b_ref, own_ref, inverse_ref, norm_ref, correlation_ref,
    partial_ref, state_ref,
    product_a_ref, product_b_ref, next_a_ref, next_b_ref, later_a_ref, later_b_ref, acc_ref, *, cols,
):
    vectors = basis_a_ref.shape[2]
    row_id = lax.axis_index("row")
    col_id = lax.axis_index("col")
    row_half = gathered_ref.shape[0] // cols // 2
    low = low_half((4, LANES))

    def place(piece):
        other_row = piece // cols
        core, rest = other_row // row_half, other_row % row_half
        return (row_id ^ (2 * rest + core)) * cols + (col_id ^ (piece % cols))

    base = 0
    for product_ref in (product_a_ref, product_b_ref):
        for index in range(product_ref.shape[0]):
            product_ref[index] = jnp.where(
                low, gathered_ref[place(base + 2 * index)], gathered_ref[place(base + 2 * index + 1)]
            )
        base += 2 * product_ref.shape[0]
    norm_now = norm_ref[pl.ds(0, 1), pl.ds(0, 1)]
    change = lane_sum(correlate([(image_a_ref, product_a_ref, 0), (image_b_ref, product_b_ref, 0)]))
    step_size = norm_now / fields_dot([(direction_a_ref, product_a_ref), (direction_b_ref, product_b_ref)])
    halves = (
        (basis_a_ref, residual_a_ref, direction_a_ref, product_a_ref, next_a_ref, later_a_ref),
        (basis_b_ref, residual_b_ref, direction_b_ref, product_b_ref, next_b_ref, later_b_ref),
    )
    for _, residual_ref, _, product_ref, next_ref, _ in halves:

        def advance(index, carry):
            next_ref[index, pl.ds(0, 3), :] = (
                residual_ref[index, pl.ds(0, 3), :] - step_size * product_ref[index, pl.ds(0, 3), :]
            )
            return carry

        run_blocks(next_ref.shape[0], advance, 0)
    norm_next = fields_dot([(next_a_ref, next_a_ref), (next_b_ref, next_b_ref)])
    correlation = correlation_ref[:, pl.ds(0, 1)] - step_size * change
    projection = lane_sum(inverse_ref[...] * row_of(correlation, identity_of(vectors)))
    momentum = norm_next / norm_now
    for basis_ref, _, direction_ref, _, next_ref, later_ref in halves:

        def point(index, carry):
            later_ref[index, pl.ds(0, 3), :] = (
                next_ref[index, pl.ds(0, 3), :]
                + momentum * direction_ref[index, pl.ds(0, 3), :]
                - combine(projection, basis_ref, index)
            )
            return carry

        run_blocks(basis_ref.shape[0], point, 0)
    product_rows(
        [(iso_a_ref, along_a_ref, info_a_ref, later_a_ref), (iso_b_ref, along_b_ref, info_b_ref, later_b_ref)],
        column_ref,
        acc_ref,
    )
    rows = rows_of_sums(acc_ref)
    width = column_ref.shape[1]
    ours = lax.broadcasted_iota(jnp.int32, (3, LANES), 1) < width
    inner = jnp.where(ours, later_a_ref[0, pl.ds(0, 3), :] * rows[:3], 0.0)
    partial = jnp.sum(lane_sum(inner), axis=0, keepdims=True)
    partial_ref[...] = jnp.broadcast_to(partial[None], partial_ref.shape)
    state_ref[pl.ds(0, 3), :] = own_ref[pl.ds(0, 3), :] + step_size * direction_a_ref[0, pl.ds(0, 3), :]
    state_ref[pl.ds(3, 3), :] = later_a_ref[0, pl.ds(0, 3), :]
    state_ref[pl.ds(6, 3), :] = next_a_ref[0, pl.ds(0, 3), :]
    state_ref[pl.ds(9, 3), :] = rows[:3]
    state_ref[pl.ds(12, 4), :] = jnp.broadcast_to(norm_next, (4, LANES))


def last_kernel(partial_ref, state_ref, solution_ref, residual_ref):
    width = solution_ref.shape[1]
    total = jnp.sum(partial_ref[...], axis=0)[:, :1]
    step_size = state_ref[pl.ds(12, 1), pl.ds(0, 1)] / total
    moved = state_ref[pl.ds(0, 3), :] + step_size * state_ref[pl.ds(3, 3), :]
    left = state_ref[pl.ds(6, 3), :] - step_size * state_ref[pl.ds(9, 3), :]
    solution_ref[...] = moved[:, :width]
    residual_ref[...] = left[:, :width]


def gather_pieces(piece, rows, cols):
    def spread(stack, axis_name, size, offsets):
        parts = [stack]
        for offset in offsets:
            parts.append(lax.ppermute(stack, axis_name, [(i, i ^ offset) for i in range(size)]))
        return jnp.concatenate(parts, axis=0)

    stack = spread(piece[None], "col", cols, range(1, cols))
    stack = spread(stack, "row", rows, range(2, rows, 2))
    return stack, lax.ppermute(stack, "row", [(i, i ^ 1) for i in range(rows)])


def exchange(stack):
    return lax.all_to_all(stack, AXES, 0, 0, tiled=True)


def body(positions, radii, basis, rhs):
    rows, cols = lax.axis_size("row"), lax.axis_size("col")
    devices = rows * cols
    blocks = devices // 4
    width = positions.shape[1]
    vectors = basis.shape[0]
    half = vectors // 2
    vmem = pl.BlockSpec(memory_space=pltpu.VMEM)

    def shaped(*shape, dtype=jnp.float32):
        return jax.ShapeDtypeStruct(shape, dtype)

    def call(kernel, name, outs, args, scratch=(), space=vmem):
        held = sum(4 * math.prod(leaf.shape) for leaf in jax.tree.leaves((outs, args, list(scratch))))
        return pl.pallas_call(
            kernel,
            name=name,
            out_shape=outs,
            in_specs=[space] * len(args),
            out_specs=jax.tree.map(lambda _: vmem, outs),
            scratch_shapes=list(scratch),
            compiler_params=pltpu.CompilerParams(vmem_limit_bytes=held * 5 // 4 + (4 << 20)),
        )(*args)

    inputs = (positions, radii[None], basis.transpose(1, 0, 2), rhs)
    packed = call(
        pack_kernel,
        "pack_inputs",
        shaped(3 * half + 8, LANES),
        tuple(pltpu.with_memory_space_constraint(array, pltpu.HBM) for array in inputs),
        [
            pltpu.VMEM((8, width), jnp.float32),
            pltpu.VMEM((3, vectors, width), jnp.float32),
            pltpu.SemaphoreType.DMA((4,)),
        ],
        space=pl.BlockSpec(memory_space=pltpu.HBM),
    )
    gathered_a, gathered_b = gather_pieces(packed, rows, cols)
    slabs = (
        shaped(blocks, width, LANES),
        shaped(blocks, width, LANES),
        shaped(blocks, 3, vectors, LANES),
        shaped(blocks // 2, 3 * vectors, 6 * LANES, dtype=jnp.bfloat16),
        shaped(blocks, 8, LANES),
    )
    tensors = [pltpu.VMEM((3 * width, 6 * LANES), jnp.bfloat16) for _ in range(2)]
    partial_shape = (3 * vectors, 3 * width)
    part, iso_a, along_a, basis_a, split_a, info_a, column = call(
        functools.partial(image_kernel, own=True),
        "image_near",
        (shaped(*partial_shape),) + slabs + (shaped(5, width, LANES),),
        (gathered_a,),
        tensors,
    )
    packed_image, iso_b, along_b, basis_b, split_b, info_b = call(
        functools.partial(image_kernel, own=False),
        "image_far",
        (shaped(3 * half, LANES),) + slabs,
        (gathered_b, part, column),
        [pltpu.VMEM(partial_shape, jnp.float32)] + tensors,
    )
    gathered_a, gathered_b = gather_pieces(packed_image, rows, cols)
    gram_shape = (3 * vectors, 3 * vectors)
    image_a, gram_part, load = call(
        functools.partial(gram_kernel, own=True),
        "gram_near",
        (shaped(blocks, 3, vectors, LANES), shaped(*gram_shape), shaped(vectors, LANES)),
        (gathered_a, split_a, basis_a, basis_b, info_a, info_b),
    )
    field = shaped(blocks, 4, LANES)
    fields = [pltpu.VMEM((blocks, 4, LANES), jnp.float32) for _ in range(6)]
    lanes_acc = pltpu.VMEM((3, width, LANES), jnp.float32)
    pairs = (basis_a, basis_b, info_a, info_b, iso_a, iso_b, along_a, along_b, column)
    product, image_b, *state = call(
        first_kernel,
        "first_product",
        (
            shaped(devices, 4, LANES),
            shaped(blocks, 3, vectors, LANES),
            field, field, field, field,
            shaped(4, LANES),
            shaped(vectors, vectors),
            shaped(8, LANES),
            shaped(vectors, LANES),
        ),
        (gathered_b, split_b, gram_part, load, image_a) + pairs,
        [pltpu.VMEM(gram_shape, jnp.float32), lanes_acc],
    )
    product = exchange(product)
    partial, state = call(
        functools.partial(second_kernel, cols=cols),
        "second_product",
        (shaped(devices, 1, LANES), shaped(16, LANES)),
        (product, image_a, image_b) + pairs + tuple(state),
        fields + [lanes_acc],
    )
    partial = exchange(partial)
    return call(last_kernel, "last_step", (shaped(3, width), shaped(3, width)), (partial, state))


def solution(mesh):
    return jax.shard_map(
        body,
        mesh=mesh,
        in_specs=(
            P(None, AXES),
            P(AXES),
            P(None, None, AXES),
            P(None, AXES),
        ),
        out_specs=(P(None, AXES), P(None, AXES)),
        check_vma=False,
    )
```

```python
import functools
import math

import jax
import jax.numpy as jnp
from jax import lax
from jax.experimental import pallas as pl
from jax.experimental.pallas import tpu as pltpu
from jax.sharding import PartitionSpec as P

LANES = 128
AXES = ("row", "col")

far_scale = 1.0 / (8.0 * math.pi)
self_scale = 1.0 / (6.0 * math.pi)
highest = lax.Precision.HIGHEST


def nt_dot(left, right, precision=highest):
    return lax.dot_general(
        left, right, (((1,), (1,)), ((), ())), precision=precision, preferred_element_type=jnp.float32
    )


def join_lanes(left, right):
    return jnp.concatenate([left, right], axis=1)


def low_half(shape):
    return lax.broadcasted_iota(jnp.int32, shape, 1) < LANES // 2


def run_blocks(count, body, carry=None):
    if count <= 16:
        for index in range(count):
            carry = body(index, carry)
        return carry
    return lax.fori_loop(0, count, body, carry)


def split(value, parts):
    pieces = []
    for part in range(parts):
        piece = value.astype(jnp.bfloat16)
        pieces.append(piece)
        if part + 1 < parts:
            value = value - piece.astype(jnp.float32)
    return pieces


def pack_kernel(pos_ref, rad_ref, basis_ref, rhs_ref, out_ref, rows_ref, fields_ref, sems):
    copies = [
        pltpu.make_async_copy(source, target, sems.at[index])
        for index, (source, target) in enumerate(
            (
                (basis_ref, fields_ref),
                (pos_ref, rows_ref.at[pl.ds(0, 3)]),
                (rad_ref, rows_ref.at[pl.ds(3, 1)]),
                (rhs_ref, rows_ref.at[pl.ds(4, 3)]),
            )
        )
    ]
    for copy in copies:
        copy.start()
    for copy in copies:
        copy.wait()
    half = fields_ref.shape[1] // 2
    for axis_id in range(3):
        piece = fields_ref[axis_id]
        out_ref[pl.ds(axis_id * half, half), :] = join_lanes(piece[:half], piece[half:])
    rows_ref[pl.ds(7, 1), :] = rows_ref[pl.ds(3, 1), :] * rows_ref[pl.ds(3, 1), :]
    rows = rows_ref[...]
    out_ref[pl.ds(3 * half, 8), :] = join_lanes(rows, rows)


def unpack_basis(first, second, half):
    low = low_half((half, LANES))
    upper = jnp.where(low, first, pltpu.roll(second, LANES // 2, 1))
    lower = jnp.where(low, pltpu.roll(first, LANES // 2, 1), second)
    return jnp.concatenate([upper, lower], axis=0)


def chunk_of(ref, index):
    return jnp.concatenate(
        [ref[2 * index + slot, axis_id] for axis_id in range(3) for slot in range(2)], axis=1
    )


def image_kernel(*refs, own):
    if own:
        gathered_ref, part_ref, iso_ref, along_ref, basis_ref, split_ref, info_ref, column_ref = refs[:8]
    else:
        gathered_ref, before_ref, column_ref = refs[:3]
        packed_ref, iso_ref, along_ref, basis_ref, split_ref, info_ref, part_ref = refs[3:10]
    high_ref, rest_ref = refs[-2:]
    blocks, width, _ = iso_ref.shape
    half = basis_ref.shape[2] // 2
    low8 = low_half((8, LANES))
    if own:
        columns = jnp.transpose(
            jnp.concatenate(
                [gathered_ref[0, pl.ds(3 * half, 8), :], jnp.zeros((LANES - 8, LANES), jnp.float32)], axis=0
            )
        )
        for slot, entry in enumerate((0, 1, 2, 7, 3)):
            column_ref[slot] = jnp.broadcast_to(columns[:width, entry : entry + 1], (width, LANES))
        part_ref[...] = jnp.zeros_like(part_ref)
    else:
        part_ref[...] = before_ref[...]

    def build(index, slot):
        first = gathered_ref.at[2 * index]
        second = gathered_ref.at[2 * index + 1]
        for axis_id in range(3):
            rows = pl.ds(axis_id * half, half)
            basis_ref[index, axis_id] = unpack_basis(first[rows, :], second[rows, :], half)
        rows = pl.ds(3 * half, 8)
        info_ref[index] = jnp.where(low8, first[rows, :], second[rows, :])
        source = [info_ref[index, pl.ds(entry, 1), :] for entry in (0, 1, 2, 7)]
        for group in range(width // 16):
            rows = pl.ds(group * 16, 16)
            deltas = [column_ref[entry, rows, :] - source[entry] for entry in range(3)]
            dist_sq = deltas[0] * deltas[0] + deltas[1] * deltas[1] + deltas[2] * deltas[2]
            check = own and not (isinstance(index, int) and index > 0)
            if check:
                lane = lax.broadcasted_iota(jnp.int32, (16, LANES), 1)
                row = lax.broadcasted_iota(jnp.int32, (16, LANES), 0) + group * 16
                coincide = lane == row
                if not isinstance(index, int):
                    coincide = coincide & (index == 0)
                dist_sq = jnp.where(coincide, 1.0, dist_sq)
            inv_dist = lax.rsqrt(dist_sq)
            inv_sq = inv_dist * inv_dist
            scaled = far_scale * inv_dist
            ratio = (column_ref[3, rows, :] + source[3]) * inv_sq
            isotropic = scaled + scaled * (ratio * (1.0 / 3.0))
            along = (scaled - scaled * ratio) * inv_sq
            if check:
                isotropic = jnp.where(coincide, self_scale / column_ref[4, rows, :], isotropic)
                along = jnp.where(coincide, 0.0, along)
            iso_ref[index, rows, :] = isotropic
            along_ref[index, rows, :] = along
            for one in range(3):
                leaning = along * deltas[one]
                for two in range(one, 3):
                    entry = leaning * deltas[two]
                    if one == two:
                        entry = entry + isotropic
                    pieces = split(entry, 2)
                    for out_axis, in_axis in sorted({(one, two), (two, one)}):
                        place = (
                            pl.ds(out_axis * width + group * 16, 16),
                            pl.ds((in_axis * 2 + slot) * LANES, LANES),
                        )
                        high_ref[place] = pieces[0]
                        rest_ref[place] = pieces[1]

    def chunk(index, _):
        build(2 * index, 0)
        build(2 * index + 1, 1)
        fields = jnp.concatenate(split(chunk_of(basis_ref, index), 3), axis=0)
        split_ref[index] = fields
        part_ref[...] += nt_dot(fields, high_ref[...], None) + nt_dot(fields, rest_ref[...], None)
        return _

    run_blocks(blocks // 2, chunk, 0)
    if not own:
        total = part_ref[...]
        image = total[: 2 * half] + total[2 * half : 4 * half] + total[4 * half :]
        for axis_id in range(3):
            piece = image[:, axis_id * width : (axis_id + 1) * width]
            packed_ref[pl.ds(axis_id * half, half), :] = join_lanes(piece[:half], piece[half:])


def row_of(column, identity):
    return jnp.sum(identity * column, axis=0, keepdims=True)


def identity_of(order):
    return jnp.where(
        lax.broadcasted_iota(jnp.int32, (order, order), 0) == lax.broadcasted_iota(jnp.int32, (order, order), 1),
        1.0,
        0.0,
    )


def invert(matrix):
    order = matrix.shape[0]
    strip = math.gcd(order, 16)
    lane = lax.broadcasted_iota(jnp.int32, (order, order), 1)
    sub = lax.broadcasted_iota(jnp.int32, (order, order), 0)
    for base in range(0, order, strip):
        columns = [
            jnp.broadcast_to(matrix[:, base + entry : base + entry + 1], (order, order)) for entry in range(strip)
        ]
        for entry in range(strip):
            step = base + entry
            column = columns[entry]
            scale = 1.0 / column[step : step + 1]
            scaled_row = jnp.where(lane[:1] == step, 1.0, matrix[step : step + 1, :]) * scale
            others = jnp.where(lane == step, 0.0, matrix) - column * scaled_row
            matrix = jnp.where(sub == step, scaled_row, others)
            for later in range(entry + 1, strip):
                pivot = columns[later][step : step + 1] * scale
                columns[later] = jnp.where(sub == step, pivot, columns[later] - column * pivot)
    return matrix


def product_rows(pairs, column_ref, acc_ref):
    width = column_ref.shape[1]
    totals = tuple(jnp.zeros((width, LANES), jnp.float32) for _ in range(3))
    for iso_ref, along_ref, info_ref, field_ref in pairs:

        def block(index, sums):
            deltas = [column_ref[entry] - info_ref[index, pl.ds(entry, 1), :] for entry in range(3)]
            field = [field_ref[index, pl.ds(entry, 1), :] for entry in range(3)]
            inner = deltas[0] * field[0] + deltas[1] * field[1] + deltas[2] * field[2]
            inner = inner * along_ref[index]
            isotropic = iso_ref[index]
            return tuple(sums[entry] + (isotropic * field[entry] + inner * deltas[entry]) for entry in range(3))

        totals = run_blocks(iso_ref.shape[0], block, totals)
    for entry in range(3):
        acc_ref[entry] = totals[entry]


def rows_of_sums(acc_ref):
    width = acc_ref.shape[1]
    ones = jnp.ones((8, LANES), jnp.float32)
    parts = [nt_dot(ones, acc_ref[entry]) for entry in range(3)]
    sub = lax.broadcasted_iota(jnp.int32, (8, width), 0)
    rows = jnp.where(sub == 0, parts[0], jnp.where(sub == 1, parts[1], jnp.where(sub == 2, parts[2], 0.0)))
    return join_lanes(rows, rows)


def correlate(pairs):
    total = None
    for image_ref, field_ref, row in pairs:

        def block(index, carry):
            for axis_id in range(3):
                carry = carry + image_ref[index, axis_id] * field_ref[index, pl.ds(row + axis_id, 1), :]
            return carry

        if total is None:
            total = jnp.zeros((image_ref.shape[2], LANES), jnp.float32)
        total = run_blocks(image_ref.shape[0], block, total)
    return total


def lane_sum(value):
    return jnp.sum(value, axis=1, keepdims=True)


def fields_dot(pairs):
    total = jnp.zeros((3, LANES), jnp.float32)
    for left_ref, right_ref in pairs:

        def block(index, carry):
            return carry + left_ref[index, pl.ds(0, 3), :] * right_ref[index, pl.ds(0, 3), :]

        total = run_blocks(left_ref.shape[0], block, total)
    return jnp.sum(lane_sum(total), axis=0, keepdims=True)


def combine(column, fields_ref, index):
    return jnp.concatenate(
        [jnp.sum(column * fields_ref[index, axis_id], axis=0, keepdims=True) for axis_id in range(3)], axis=0
    )


def gram_kernel(gathered_ref, split_ref, *refs, own):
    if own:
        basis_refs, info_refs = refs[:2], refs[2:4]
        image_ref, part_ref, load_ref = refs[4:7]
    else:
        image_ref, part_ref = refs
    blocks = image_ref.shape[0]
    vectors = image_ref.shape[2]
    half = vectors // 2

    def chunk(index, carry):
        for slot in range(2):
            for axis_id in range(3):
                rows = pl.ds(axis_id * half, half)
                image_ref[2 * index + slot, axis_id] = unpack_basis(
                    gathered_ref[4 * index + 2 * slot, rows, :],
                    gathered_ref[4 * index + 2 * slot + 1, rows, :],
                    half,
                )
        images = jnp.concatenate(split(chunk_of(image_ref, index), 3), axis=0)
        return carry + nt_dot(split_ref[index], images, None)

    part_ref[...] = run_blocks(blocks // 2, chunk, jnp.zeros((3 * vectors, 3 * vectors), jnp.float32))
    if own:
        load_ref[...] = correlate([(basis_refs[0], info_refs[0], 4), (basis_refs[1], info_refs[1], 4)])


def first_kernel(
    gathered_ref, split_ref, before_ref, load_ref, image_a_ref, basis_a_ref, basis_b_ref, info_a_ref, info_b_ref,
    iso_a_ref, iso_b_ref, along_a_ref, along_b_ref, column_ref,
    rows_ref, image_b_ref, residual_a_ref, residual_b_ref, direction_a_ref, direction_b_ref, own_ref, inverse_ref,
    norm_ref, correlation_ref, part_ref, acc_ref,
):
    vectors = basis_a_ref.shape[2]
    gram_kernel(gathered_ref, split_ref, image_b_ref, part_ref, own=False)
    part = part_ref[...] + before_ref[...]
    part = part[:vectors] + part[vectors : 2 * vectors] + part[2 * vectors :]
    gram = part[:, :vectors] + part[:, vectors : 2 * vectors] + part[:, 2 * vectors :]
    identity = identity_of(vectors)
    inverse = invert(gram)
    inverse_ref[...] = inverse

    def coarse_solve(column):
        return lane_sum(inverse * row_of(column, identity))

    coarse = coarse_solve(lane_sum(load_ref[...]))
    halves = (
        (image_a_ref, basis_a_ref, info_a_ref, residual_a_ref, direction_a_ref),
        (image_b_ref, basis_b_ref, info_b_ref, residual_b_ref, direction_b_ref),
    )
    for image_ref, _, info_ref, residual_ref, _ in halves:

        def remain(index, carry):
            residual_ref[index, pl.ds(0, 3), :] = info_ref[index, pl.ds(4, 3), :] - combine(
                coarse, image_ref, index
            )
            return carry

        run_blocks(image_ref.shape[0], remain, 0)
    norm_ref[...] = jnp.broadcast_to(
        fields_dot([(residual_a_ref, residual_a_ref), (residual_b_ref, residual_b_ref)]), norm_ref.shape
    )
    correlation = lane_sum(correlate([(image_a_ref, residual_a_ref, 0), (image_b_ref, residual_b_ref, 0)]))
    correlation_ref[...] = jnp.broadcast_to(correlation, correlation_ref.shape)
    projection = coarse_solve(correlation)
    for _, basis_ref, _, residual_ref, direction_ref in halves:

        def point(index, carry):
            direction_ref[index, pl.ds(0, 3), :] = residual_ref[index, pl.ds(0, 3), :] - combine(
                projection, basis_ref, index
            )
            return carry

        run_blocks(basis_ref.shape[0], point, 0)
    own_ref[pl.ds(0, 3), :] = combine(coarse, basis_a_ref, 0)
    product_rows(
        [
            (iso_a_ref, along_a_ref, info_a_ref, direction_a_ref),
            (iso_b_ref, along_b_ref, info_b_ref, direction_b_ref),
        ],
        column_ref,
        acc_ref,
    )
    rows = rows_of_sums(acc_ref)[:4]
    rows_ref[...] = jnp.broadcast_to(rows[None], rows_ref.shape)


def second_kernel(
    gathered_ref, image_a_ref, image_b_ref, basis_a_ref, basis_b_ref, info_a_ref, info_b_ref,
    iso_a_ref, iso_b_ref, along_a_ref, along_b_ref, column_ref,
    residual_a_ref, residual_b_ref, direction_a_ref, direction_b_ref, own_ref, inverse_ref, norm_ref, correlation_ref,
    partial_ref, state_ref,
    product_a_ref, product_b_ref, next_a_ref, next_b_ref, later_a_ref, later_b_ref, acc_ref, *, cols,
):
    vectors = basis_a_ref.shape[2]
    row_id = lax.axis_index("row")
    col_id = lax.axis_index("col")
    row_half = gathered_ref.shape[0] // cols // 2
    low = low_half((4, LANES))

    def place(piece):
        other_row = piece // cols
        core, rest = other_row // row_half, other_row % row_half
        return (row_id ^ (2 * rest + core)) * cols + (col_id ^ (piece % cols))

    base = 0
    for product_ref in (product_a_ref, product_b_ref):
        for index in range(product_ref.shape[0]):
            product_ref[index] = jnp.where(
                low, gathered_ref[place(base + 2 * index)], gathered_ref[place(base + 2 * index + 1)]
            )
        base += 2 * product_ref.shape[0]
    norm_now = norm_ref[pl.ds(0, 1), pl.ds(0, 1)]
    change = lane_sum(correlate([(image_a_ref, product_a_ref, 0), (image_b_ref, product_b_ref, 0)]))
    step_size = norm_now / fields_dot([(direction_a_ref, product_a_ref), (direction_b_ref, product_b_ref)])
    halves = (
        (basis_a_ref, residual_a_ref, direction_a_ref, product_a_ref, next_a_ref, later_a_ref),
        (basis_b_ref, residual_b_ref, direction_b_ref, product_b_ref, next_b_ref, later_b_ref),
    )
    for _, residual_ref, _, product_ref, next_ref, _ in halves:

        def advance(index, carry):
            next_ref[index, pl.ds(0, 3), :] = (
                residual_ref[index, pl.ds(0, 3), :] - step_size * product_ref[index, pl.ds(0, 3), :]
            )
            return carry

        run_blocks(next_ref.shape[0], advance, 0)
    norm_next = fields_dot([(next_a_ref, next_a_ref), (next_b_ref, next_b_ref)])
    correlation = correlation_ref[:, pl.ds(0, 1)] - step_size * change
    projection = lane_sum(inverse_ref[...] * row_of(correlation, identity_of(vectors)))
    momentum = norm_next / norm_now
    for basis_ref, _, direction_ref, _, next_ref, later_ref in halves:

        def point(index, carry):
            later_ref[index, pl.ds(0, 3), :] = (
                next_ref[index, pl.ds(0, 3), :]
                + momentum * direction_ref[index, pl.ds(0, 3), :]
                - combine(projection, basis_ref, index)
            )
            return carry

        run_blocks(basis_ref.shape[0], point, 0)
    product_rows(
        [(iso_a_ref, along_a_ref, info_a_ref, later_a_ref), (iso_b_ref, along_b_ref, info_b_ref, later_b_ref)],
        column_ref,
        acc_ref,
    )
    rows = rows_of_sums(acc_ref)
    width = column_ref.shape[1]
    ours = lax.broadcasted_iota(jnp.int32, (3, LANES), 1) < width
    inner = jnp.where(ours, later_a_ref[0, pl.ds(0, 3), :] * rows[:3], 0.0)
    partial = jnp.sum(lane_sum(inner), axis=0, keepdims=True)
    partial_ref[...] = jnp.broadcast_to(partial[None], partial_ref.shape)
    state_ref[pl.ds(0, 3), :] = own_ref[pl.ds(0, 3), :] + step_size * direction_a_ref[0, pl.ds(0, 3), :]
    state_ref[pl.ds(3, 3), :] = later_a_ref[0, pl.ds(0, 3), :]
    state_ref[pl.ds(6, 3), :] = next_a_ref[0, pl.ds(0, 3), :]
    state_ref[pl.ds(9, 3), :] = rows[:3]
    state_ref[pl.ds(12, 4), :] = jnp.broadcast_to(norm_next, (4, LANES))


def last_kernel(partial_ref, state_ref, solution_ref, residual_ref):
    width = solution_ref.shape[1]
    total = jnp.sum(partial_ref[...], axis=0)[:, :1]
    step_size = state_ref[pl.ds(12, 1), pl.ds(0, 1)] / total
    moved = state_ref[pl.ds(0, 3), :] + step_size * state_ref[pl.ds(3, 3), :]
    left = state_ref[pl.ds(6, 3), :] - step_size * state_ref[pl.ds(9, 3), :]
    solution_ref[...] = moved[:, :width]
    residual_ref[...] = left[:, :width]


def gather_orders(rows, cols):
    return (("col", cols, tuple(range(cols - 1, 0, -1))), ("row", rows, tuple(range(rows - 2, 0, -2))))


def gather_pieces(piece, rows, cols):
    stack = piece[None]
    for axis_name, size, offsets in gather_orders(rows, cols):
        parts = {0: stack}
        for offset in offsets:
            parts[offset] = lax.ppermute(stack, axis_name, [(i, i ^ offset) for i in range(size)])
        stack = jnp.concatenate([parts[offset] for offset in sorted(parts)], axis=0)
    return stack, lax.ppermute(stack, "row", [(i, i ^ 1) for i in range(rows)])


def exchange(stack):
    return lax.all_to_all(stack, AXES, 0, 0, tiled=True)


def body(positions, radii, basis, rhs):
    rows, cols = lax.axis_size("row"), lax.axis_size("col")
    devices = rows * cols
    blocks = devices // 4
    width = positions.shape[1]
    vectors = basis.shape[0]
    half = vectors // 2
    vmem = pl.BlockSpec(memory_space=pltpu.VMEM)

    def shaped(*shape, dtype=jnp.float32):
        return jax.ShapeDtypeStruct(shape, dtype)

    def call(kernel, outs, args, scratch=(), space=vmem):
        held = sum(4 * math.prod(leaf.shape) for leaf in jax.tree.leaves((outs, args, list(scratch))))
        return pl.pallas_call(
            kernel,
            out_shape=outs,
            in_specs=[space] * len(args),
            out_specs=jax.tree.map(lambda _: vmem, outs),
            scratch_shapes=list(scratch),
            compiler_params=pltpu.CompilerParams(vmem_limit_bytes=held * 5 // 4 + (4 << 20)),
        )(*args)

    inputs = (positions, radii[None], basis.transpose(1, 0, 2), rhs)
    packed = call(
        pack_kernel,
        shaped(3 * half + 8, LANES),
        tuple(pltpu.with_memory_space_constraint(array, pltpu.HBM) for array in inputs),
        [
            pltpu.VMEM((8, width), jnp.float32),
            pltpu.VMEM((3, vectors, width), jnp.float32),
            pltpu.SemaphoreType.DMA((4,)),
        ],
        space=pl.BlockSpec(memory_space=pltpu.HBM),
    )
    gathered_a, gathered_b = gather_pieces(packed, rows, cols)
    slabs = (
        shaped(blocks, width, LANES),
        shaped(blocks, width, LANES),
        shaped(blocks, 3, vectors, LANES),
        shaped(blocks // 2, 3 * vectors, 6 * LANES, dtype=jnp.bfloat16),
        shaped(blocks, 8, LANES),
    )
    tensors = [pltpu.VMEM((3 * width, 6 * LANES), jnp.bfloat16) for _ in range(2)]
    partial_shape = (3 * vectors, 3 * width)
    part, iso_a, along_a, basis_a, split_a, info_a, column = call(
        functools.partial(image_kernel, own=True),
        (shaped(*partial_shape),) + slabs + (shaped(5, width, LANES),),
        (gathered_a,),
        tensors,
    )
    packed_image, iso_b, along_b, basis_b, split_b, info_b = call(
        functools.partial(image_kernel, own=False),
        (shaped(3 * half, LANES),) + slabs,
        (gathered_b, part, column),
        [pltpu.VMEM(partial_shape, jnp.float32)] + tensors,
    )
    gathered_a, gathered_b = gather_pieces(packed_image, rows, cols)
    gram_shape = (3 * vectors, 3 * vectors)
    image_a, gram_part, load = call(
        functools.partial(gram_kernel, own=True),
        (shaped(blocks, 3, vectors, LANES), shaped(*gram_shape), shaped(vectors, LANES)),
        (gathered_a, split_a, basis_a, basis_b, info_a, info_b),
    )
    field = shaped(blocks, 4, LANES)
    fields = [pltpu.VMEM((blocks, 4, LANES), jnp.float32) for _ in range(6)]
    lanes_acc = pltpu.VMEM((3, width, LANES), jnp.float32)
    pairs = (basis_a, basis_b, info_a, info_b, iso_a, iso_b, along_a, along_b, column)
    product, image_b, *state = call(
        first_kernel,
        (
            shaped(devices, 4, LANES),
            shaped(blocks, 3, vectors, LANES),
            field, field, field, field,
            shaped(4, LANES),
            shaped(vectors, vectors),
            shaped(8, LANES),
            shaped(vectors, LANES),
        ),
        (gathered_b, split_b, gram_part, load, image_a) + pairs,
        [pltpu.VMEM(gram_shape, jnp.float32), lanes_acc],
    )
    product = exchange(product)
    partial, state = call(
        functools.partial(second_kernel, cols=cols),
        (shaped(devices, 1, LANES), shaped(16, LANES)),
        (product, image_a, image_b) + pairs + tuple(state),
        fields + [lanes_acc],
    )
    partial = exchange(partial)
    return call(last_kernel, (shaped(3, width), shaped(3, width)), (partial, state))


def solution(mesh):
    return jax.shard_map(
        body,
        mesh=mesh,
        in_specs=(
            P(None, AXES),
            P(AXES),
            P(None, None, AXES),
            P(None, AXES),
        ),
        out_specs=(P(None, AXES), P(None, AXES)),
        check_vma=False,
    )
```
